32 devices in a mesh: groups: 2 (over y), expert: 8 (over z, x), dp: 2 (over core).
Axes of the slice: x: 2, y: 2, z: 4, core: 2. Of those that a mesh axis runs over, the one named last changes fastest.
Arguments:
- tokens: bfloat16 [4096, 2048], P(('groups', 'expert', 'dp')), parts along dimension 0, may hold values from -6 to 6
- cotangent: bfloat16 [4096, 2048], P(('groups', 'expert', 'dp')), parts along dimension 0, may hold values from -6 to 6
- routes: int32 [4096, 4], P(('groups', 'expert', 'dp')), parts along dimension 0, may hold values from 0 to 15, as said below
- gates: float32 [4096, 4], P(('groups', 'expert', 'dp')), parts along dimension 0, may hold values from 0.05 to 0.6
- helper: int32 [32], P('groups'), parts along dimension 0, may hold values from 0 to 1
- w_gate: bfloat16 [16, 2048, 384], P(('expert', 'dp')), may hold values from -0.125 to 0.125
- w_up: bfloat16 [16, 2048, 384], P(('expert', 'dp')), may hold values from -0.125 to 0.125
- w_down: bfloat16 [16, 384, 2048], P(('expert', 'dp')), may hold values from -0.3125 to 0.3125
Outputs:
- grad_tokens: bfloat16 [4096, 2048], P(('groups', 'expert', 'dp')), parts along dimension 0
- grad_gate: bfloat16 [32, 2048, 384], P(('groups', 'expert', 'dp')), parts along dimension 0
- grad_up: bfloat16 [32, 2048, 384], P(('groups', 'expert', 'dp')), parts along dimension 0
- grad_down: bfloat16 [32, 384, 2048], P(('groups', 'expert', 'dp')), parts along dimension 0
The draws below stay inside these ranges and needn't reach their ends.
There are 2 independent parts, one for each index of `groups`. The reference program is written for one: setup_inputs(seed, part) draws one part's arguments, and reference() takes and returns one part's arrays. A program takes and returns all parts, laid end to end along the dimension named above; an argument that names none is the same for every part. Nothing has to cross between parts.
Inputs may be any that keep to these rules, and one draw needn't show every extreme that they name: `routes`: each row names 4 different experts; the rows of one device name no expert more than 64 times, and some expert exactly 64 times in the rows of every device.
All inputs are finite; a program needn't handle non-finite values.
Results may differ from the reference program's by a relative error of at most 0.0065.
Values may be sent and summed in bfloat16 or wider, within the bound.
A program may use at most 128 MiB of HBM per device.

```python
import math
import jax
import jax.numpy as jnp
from jax import lax

D = 2048
HIDDEN_SIZE = 384
TOP_K = 4
TOK_DEV = 128
EXPERTS = 16
TOKENS = 2048
ROUTE_CAP = 64
HOME_CAP = 40


def expert_order(key):
    return jax.random.permutation(jax.random.fold_in(key, 7), EXPERTS).astype(jnp.int32)


def draw_routes(key, part):
    order = expert_order(key)
    busiest = max(1, EXPERTS // 16)
    block_rows = TOK_DEV * TOP_K
    spare = block_rows - busiest * ROUTE_CAP
    others = EXPERTS - busiest
    spread = max(0, (spare // others - 1) // 2)

    def one_block(block):
        block_key = jax.random.fold_in(jax.random.fold_in(key, 13), block)
        key_edge, key_cold, key_group, key_token = jax.random.split(block_key, 4)
        edges = jnp.arange(others + 1, dtype=jnp.int32) * spare // others
        jitter = jax.random.randint(key_edge, (others + 1,), -spread, spread + 1).astype(jnp.int32)
        jitter = jitter.at[0].set(0).at[others].set(0)
        edges = edges + jitter
        cold_sizes = edges[1:] - edges[:-1]
        cold_perm = jax.random.permutation(key_cold, others)
        counts = jnp.zeros((EXPERTS,), jnp.int32).at[order[:busiest]].set(ROUTE_CAP)
        counts = counts.at[order[busiest:][cold_perm]].set(cold_sizes)
        group = jax.random.permutation(key_group, EXPERTS).astype(jnp.int32)
        bounds = jnp.cumsum(counts[group])
        place = jnp.arange(block_rows, dtype=jnp.int32)
        which = jnp.searchsorted(bounds, place, side='right')
        layout = group[which]
        grid = layout.reshape(TOP_K, TOK_DEV).T
        token_perm = jax.random.permutation(key_token, TOK_DEV)
        return jnp.zeros_like(grid).at[token_perm].set(grid)
    blocks = jax.vmap(one_block)(jnp.arange(EXPERTS, dtype=jnp.int32))
    return blocks.reshape(TOKENS, TOP_K).astype(jnp.int32)


def draw_helper(key, part):
    order = expert_order(key)
    flags = jax.random.randint(jax.random.fold_in(key, 17), (EXPERTS,), 0, 2).astype(jnp.int32)
    flags = flags.at[jnp.bitwise_xor(order[0], 1)].set(1)
    if max(1, EXPERTS // 16) > 1:
        flags = flags.at[jnp.bitwise_xor(order[1], 1)].set(0)
    return flags.astype(jnp.int32)


def level_of(own_key, extent, cuts, smallest, largest):
    level, own = 1.0, jax.random.fold_in(own_key, 6)
    for axis_at, shards_of in cuts:
        draws = jnp.exp(jax.random.uniform(jax.random.fold_in(own, axis_at), (shards_of,), jnp.float32, smallest / len(cuts), largest / len(cuts)))
        level = level * jnp.repeat(draws, extent[axis_at] // shards_of).reshape([-1 if axis == axis_at else 1 for axis in range(len(extent))])
    return level


def scatter_about(own_key, dims, scale, limit, pieces=(), kind=jnp.bfloat16):
    level = level_of(own_key, dims, pieces, -0.22, 0.18) if pieces else 1.0
    drawn = jax.random.normal(own_key, dims, jnp.float32) * scale * level
    return jnp.minimum(jnp.maximum(drawn, -limit), limit).astype(kind)


def setup_inputs(seed: int = 0, part: int = 0) -> dict:
    arg_keys = jax.random.split(jax.random.key(seed), 9)
    own_keys = jax.random.split(jax.random.fold_in(arg_keys[8], part), 9)
    tokens = scatter_about(own_keys[0], (TOKENS, D), 1.0, 6.0, ((0, 16),))
    cotangent = scatter_about(own_keys[1], (TOKENS, D), 0.5, 6.0, ((0, 16),))
    routes = draw_routes(jax.random.fold_in(jax.random.fold_in(arg_keys[8], part), 71), part)
    gates = jnp.clip(jnp.exp(math.log(0.6) - 2.4849067 * jax.random.uniform(own_keys[3], (TOKENS, TOP_K), jnp.float32) ** level_of(own_keys[3], (TOKENS, TOP_K), ((0, 16),), -0.2, 0.2)), 0.05, 0.6)
    helper = draw_helper(jax.random.fold_in(jax.random.fold_in(arg_keys[8], part), 71), part)
    w_gate = scatter_about(arg_keys[5], (EXPERTS, D, HIDDEN_SIZE), D ** -0.5, 0.125, ((0, 16),))
    w_up = scatter_about(arg_keys[6], (EXPERTS, D, HIDDEN_SIZE), D ** -0.5, 0.125, ((0, 16),))
    w_down = scatter_about(arg_keys[7], (EXPERTS, HIDDEN_SIZE, D), HIDDEN_SIZE ** -0.5, 0.3125, ((0, 16),))
    return dict(tokens=tokens, cotangent=cotangent, routes=routes, gates=gates, helper=helper, w_gate=w_gate, w_up=w_up, w_down=w_down)


def expert_pass(rows, scaled, gate_w, up_w, down_w):
    gate_pre = jnp.dot(rows, gate_w, preferred_element_type=jnp.float32)
    up_pre = jnp.dot(rows, up_w, preferred_element_type=jnp.float32)
    sigma = jax.nn.sigmoid(gate_pre)
    active = gate_pre * sigma
    hidden = (active * up_pre).astype(jnp.bfloat16)
    over_last = (((1,), (1,)), ((), ()))
    over_rows = (((0,), (0,)), ((), ()))
    back_hidden = lax.dot_general(scaled, down_w, over_last, preferred_element_type=jnp.float32)
    grad_gating = (back_hidden * up_pre * sigma * (1.0 + gate_pre * (1.0 - sigma))).astype(jnp.bfloat16)
    grad_upward = (back_hidden * active).astype(jnp.bfloat16)
    grad_down = lax.dot_general(hidden, scaled, over_rows, preferred_element_type=jnp.float32)
    grad_gate = lax.dot_general(rows, grad_gating, over_rows, preferred_element_type=jnp.float32)
    grad_up = lax.dot_general(rows, grad_upward, over_rows, preferred_element_type=jnp.float32)
    row_grads = lax.dot_general(grad_gating, gate_w, over_last, preferred_element_type=jnp.float32)
    row_grads = row_grads + lax.dot_general(grad_upward, up_w, over_last, preferred_element_type=jnp.float32)
    return row_grads.astype(jnp.bfloat16), grad_gate, grad_up, grad_down


def reference(tokens, cotangent, routes, gates, helper, w_gate, w_up, w_down):
    block_rows = TOK_DEV * TOP_K
    routes_all = TOKENS * TOP_K
    experts_row = jnp.arange(EXPERTS, dtype=jnp.int32)

    def block_rank(block_ids):
        one_hot = (block_ids[:, None] == experts_row[None, :]).astype(jnp.float32)
        before = jnp.cumsum(one_hot, axis=0) - one_hot
        return jnp.sum(before * one_hot, axis=1).astype(jnp.int32)

    route_rank = lax.map(block_rank, routes.reshape(EXPERTS, block_rows)).reshape(routes_all)
    flat_ids = routes.reshape(routes_all)
    partner_flag = helper[jnp.bitwise_xor(flat_ids, 1)]
    kept = (route_rank < HOME_CAP) | (partner_flag == 1)
    route_index = jnp.arange(routes_all, dtype=jnp.int32)
    column = (route_index // block_rows) * ROUTE_CAP + route_rank
    row_target = jnp.where(kept, flat_ids, EXPERTS).astype(jnp.int32)
    table = jnp.full((EXPERTS, EXPERTS * ROUTE_CAP), routes_all, jnp.int32)
    table = table.at[row_target, column].set(route_index, mode="drop")
    tokens_pad = jnp.concatenate([tokens, jnp.zeros((1, D), jnp.bfloat16)], axis=0)
    cot_pad = jnp.concatenate([cotangent, jnp.zeros((1, D), jnp.bfloat16)], axis=0)
    gate_pad = jnp.concatenate([gates.reshape(routes_all), jnp.zeros((1,), jnp.float32)], axis=0)

    def per_expert(carry, inputs):
        source, gate_w, up_w, down_w = inputs
        token_of = jnp.where(source < routes_all, source // TOP_K, TOKENS).astype(jnp.int32)
        rows = tokens_pad[token_of]
        scaled = (cot_pad[token_of].astype(jnp.float32) * gate_pad[source][:, None]).astype(jnp.bfloat16)
        row_grads, grad_gate, grad_up, grad_down = expert_pass(rows, scaled, gate_w, up_w, down_w)
        carry = carry.at[token_of].add(row_grads.astype(jnp.float32))
        return carry, (grad_gate.astype(jnp.bfloat16), grad_up.astype(jnp.bfloat16), grad_down.astype(jnp.bfloat16))

    start = jnp.zeros((TOKENS + 1, D), jnp.float32)
    final, stacked = lax.scan(per_expert, start, (table, w_gate, w_up, w_down))
    return final[:TOKENS].astype(jnp.bfloat16), stacked[0], stacked[1], stacked[2]
```

```python
import functools

import jax
import jax.numpy as jnp
from jax import lax
from jax.experimental import pallas as pl
from jax.experimental.pallas import tpu as pltpu
from jax.sharding import PartitionSpec as P

MESH = pl.DeviceIdType.MESH
BF16 = jnp.bfloat16
F32 = jnp.float32


def expert_pass(rows, scaled, gate_w, up_w, down_w):
    gate_pre = jnp.dot(rows, gate_w, preferred_element_type=jnp.float32)
    up_pre = jnp.dot(rows, up_w, preferred_element_type=jnp.float32)
    sigma = jax.nn.sigmoid(gate_pre)
    active = gate_pre * sigma
    hidden = (active * up_pre).astype(jnp.bfloat16)
    over_last = (((1,), (1,)), ((), ()))
    over_rows = (((0,), (0,)), ((), ()))
    back_hidden = lax.dot_general(scaled, down_w, over_last, preferred_element_type=jnp.float32)
    grad_gating = (back_hidden * up_pre * sigma * (1.0 + gate_pre * (1.0 - sigma))).astype(
        jnp.bfloat16
    )
    grad_upward = (back_hidden * active).astype(jnp.bfloat16)
    grad_down = lax.dot_general(hidden, scaled, over_rows, preferred_element_type=jnp.float32)
    grad_gate = lax.dot_general(rows, grad_gating, over_rows, preferred_element_type=jnp.float32)
    grad_up = lax.dot_general(rows, grad_upward, over_rows, preferred_element_type=jnp.float32)
    row_grads = lax.dot_general(grad_gating, gate_w, over_last, preferred_element_type=jnp.float32)
    row_grads = row_grads + lax.dot_general(
        grad_upward, up_w, over_last, preferred_element_type=jnp.float32
    )
    return (row_grads.astype(jnp.bfloat16), grad_gate, grad_up, grad_down)


def local(tokens, cotangent, routes, gates, helper, w_gate, w_up, w_down):
    tok_rows, width = tokens.shape
    top_count = routes.shape[1]
    devices = lax.axis_size(("expert", "dp"))
    route_cap = 2 * tok_rows * top_count // devices
    spill_cap = 3 * route_cap // 8
    home_cap = route_cap - spill_cap
    block_rows = tok_rows * top_count
    slots = devices * route_cap
    flat_ids = routes.reshape(block_rows)
    experts_row = jnp.arange(devices, dtype=jnp.int32)
    one_hot = (flat_ids[:, None] == experts_row[None, :]).astype(jnp.float32)
    positions = jnp.arange(block_rows, dtype=jnp.int32)
    lower = (positions[:, None] > positions[None, :]).astype(jnp.float32)
    before = jnp.dot(lower, one_hot, precision=lax.Precision.HIGHEST)
    route_rank = jnp.sum(before * one_hot, axis=1).astype(jnp.int32)
    partner_help = helper.reshape(devices // 2, 2)[:, ::-1].reshape(devices).astype(jnp.float32)
    helped = jnp.dot(one_hot, partner_help, precision=lax.Precision.HIGHEST) > 0.5
    spilled = route_rank >= home_cap
    kept = jnp.logical_not(spilled) | helped
    slot_index = jnp.where(kept, flat_ids * route_cap + route_rank, slots)
    source = jnp.full((slots + 1,), block_rows, jnp.int32).at[slot_index].set(positions)[:slots]
    token_of = jnp.where(source < block_rows, source // top_count, tok_rows)
    tokens_pad = jnp.concatenate([tokens, jnp.zeros((1, width), jnp.bfloat16)], axis=0)
    cot_pad = jnp.concatenate([cotangent, jnp.zeros((1, width), jnp.bfloat16)], axis=0)
    gate_pad = jnp.concatenate([gates.reshape(block_rows), jnp.zeros((1,), jnp.float32)], axis=0)
    send_rows = tokens_pad[token_of].reshape(devices, route_cap, width)
    send_scaled = (cot_pad[token_of].astype(jnp.float32) * gate_pad[source][:, None]).astype(
        jnp.bfloat16
    )
    send_scaled = send_scaled.reshape(devices, route_cap, width)
    recv_rows, recv_scaled = (
        lax.all_to_all(send_rows, ("expert", "dp"), split_axis=0, concat_axis=0, tiled=True),
        lax.all_to_all(send_scaled, ("expert", "dp"), split_axis=0, concat_axis=0, tiled=True),
    )
    gate_w = w_gate[0]
    up_w = w_up[0]
    down_w = w_down[0]
    whole_out = expert_pass(
        recv_rows.reshape(slots, width), recv_scaled.reshape(slots, width), gate_w, up_w, down_w
    )
    grad_gate = whole_out[1]
    grad_up = whole_out[2]
    grad_down = whole_out[3]
    row_grads = whole_out[0].reshape(devices, route_cap, width)
    back_rows = lax.all_to_all(row_grads, ("expert", "dp"), split_axis=0, concat_axis=0, tiled=True)
    back_pad = jnp.concatenate(
        [back_rows.reshape(slots, width), jnp.zeros((1, width), jnp.bfloat16)], axis=0
    )
    picked = back_pad[slot_index].reshape(tok_rows, top_count, width)
    grad_tokens = jnp.sum(picked.astype(jnp.float32), axis=1).astype(jnp.bfloat16)
    return (
        grad_tokens,
        grad_gate[None].astype(jnp.bfloat16),
        grad_up[None].astype(jnp.bfloat16),
        grad_down[None].astype(jnp.bfloat16),
    )


def ring_kernel(
    n, cap, home,
    tok_in, cot_in, rt_in, gt_in, help_in, wg_in, wu_in, wd_in,
    out_tok, out_gate, out_up, out_down,
    TOK, COT, RT, GT, HELP, WC, WD, R, S, H, GGU, PART, SIB, RB,
    lsem, wsem, ag_send, ag_recv, sib_send, sib_recv,
    ps_send, ps_recv, rs_send, rs_recv,
):
    half = n // 2
    rows, width = tok_in.shape
    hid = wd_in.shape[0]
    hr = rows // 2
    qr = rows // 4
    tile = width // 4
    e = lax.axis_index("expert")
    c = lax.axis_index("dp")
    z = e // 2
    x = e % 2
    pos = z + x * (n - 1 - 2 * z)

    def chip_at(q):
        q = q % n
        side = q // half
        return side * (2 * (n - 1 - q) + 1) + (1 - side) * 2 * q

    nxt = ({"expert": chip_at(pos + 1)}, {"expert": chip_at(pos + n - 1)})
    sib = {"dp": 1 - c}
    me = e * 2 + c

    def far(d):
        return pl.ds(d * hr, hr)

    local = [
        pltpu.make_async_copy(tok_in, TOK.at[0, 0], lsem.at[0]),
        pltpu.make_async_copy(cot_in, COT.at[0, 0], lsem.at[1]),
        pltpu.make_async_copy(rt_in, RT.at[0, 0], lsem.at[2]),
        pltpu.make_async_copy(gt_in, GT.at[0, 0], lsem.at[3]),
        pltpu.make_async_copy(help_in, HELP, lsem.at[4]),
    ]
    weights = [
        pltpu.make_async_copy(wg_in, WC.at[:, pl.ds(0, hid)], wsem.at[0]),
        pltpu.make_async_copy(wu_in, WC.at[:, pl.ds(hid, hid)], wsem.at[1]),
        pltpu.make_async_copy(wd_in, WD, wsem.at[2]),
    ]
    for cp in local + weights:
        cp.start()

    barrier = pltpu.get_barrier_semaphore()
    for who in (nxt[0], nxt[1], sib):
        pl.semaphore_signal(barrier, inc=1, device_id=who, device_id_type=MESH)
    pl.semaphore_wait(barrier, 3)

    bufs = (TOK, COT, RT, GT)
    own = (tok_in, cot_in, rt_in, gt_in)
    order = (2, 3, 0, 1)
    sends = []

    def put(src, dst, ssem, rsem, who):
        cp = pltpu.make_async_remote_copy(
            src_ref=src, dst_ref=dst, send_sem=ssem, recv_sem=rsem,
            device_id=who, device_id_type=MESH,
        )
        cp.start()
        sends.append(cp)

    def arrived(dst, ssem, rsem, who):
        pltpu.make_async_remote_copy(
            src_ref=dst, dst_ref=dst, send_sem=ssem, recv_sem=rsem,
            device_id=who, device_id_type=MESH,
        ).wait_recv()

    def slot(d, s):
        return (n - s) % n if d == 0 else s % n

    def piece(a, d, s):
        ref = bufs[a].at[slot(d, s), 0]
        if s == half and a < 2:
            return ref.at[far(d), :]
        return ref

    def sib_piece(a, d, s):
        ref = bufs[a].at[slot(d, s), 1]
        if s == half and a < 2:
            return ref.at[far(d), :]
        return ref

    def ring_put(a, d, s):
        if s == half and a >= 2 and d == 1:
            return
        src = own[a] if s == 1 else bufs[a].at[slot(d, s - 1), 0]
        if s == half and a < 2:
            src = src.at[far(d), :]
        put(src, piece(a, d, s), ag_send.at[a, d, s - 1], ag_recv.at[a, d, s - 1], nxt[d])

    def ring_take(a, d, s):
        if s == half and a >= 2 and d == 1:
            return
        arrived(piece(a, d, s), ag_send.at[a, d, s - 1], ag_recv.at[a, d, s - 1], nxt[d])
        if s < half:
            ring_put(a, d, s + 1)
        k = 1 + d * half + s - 1
        put(piece(a, d, s), sib_piece(a, d, s), sib_send.at[a, k], sib_recv.at[a, k], sib)

    def sib_take(a, d, s):
        if s == half and a >= 2 and d == 1:
            return
        k = 1 + d * half + s - 1
        arrived(sib_piece(a, d, s), sib_send.at[a, k], sib_recv.at[a, k], sib)

    for a in order:
        for d in (0, 1):
            ring_put(a, d, 1)
    for a in order:
        put(own[a], bufs[a].at[0, 1], sib_send.at[a, 0], sib_recv.at[a, 0], sib)

    earlier = (
        lax.broadcasted_iota(jnp.int32, (rows, rows), 0)
        < lax.broadcasted_iota(jnp.int32, (rows, rows), 1)
    ).astype(BF16)
    slot_ids = lax.broadcasted_iota(jnp.int32, (cap, rows), 0).astype(F32)
    over_last = (((1,), (1,)), ((), ()))
    over_rows = (((0,), (0,)), ((), ()))

    def token_part(blocks, base):
        partner = me + 1 - 2 * (me % 2)
        lanes = lax.broadcasted_iota(jnp.int32, HELP.shape, 1)
        flag = jnp.sum(jnp.where(lanes == partner, HELP[...], 0).astype(F32), axis=1, keepdims=True)
        limit = jnp.where(flag == 1.0, float(rows), home - 0.5)
        picks = []
        for i, (o, q) in enumerate(blocks):
            hit = RT[o, q] == me
            named = jnp.sum(hit.astype(F32), axis=0, keepdims=True)
            gate = jnp.sum(jnp.where(hit, GT[o, q], 0.0), axis=0, keepdims=True)
            named16 = jnp.broadcast_to(named, (16, rows)).astype(BF16)
            rank = jnp.dot(named16, earlier, preferred_element_type=F32)[0:1]
            kept = (named > 0.5) & (rank < limit)
            place = jnp.where(kept, rank, -1.0)
            hot = slot_ids == place
            gsel = jnp.sum(jnp.where(hot, gate, 0.0), axis=1, keepdims=True)
            hotf = hot.astype(F32)
            hotb = hotf.astype(BF16)
            picks.append((hotb, gsel, jnp.transpose(hotf).astype(BF16)))
            at = pl.ds(base + i * cap, cap)

            def gather(j, _, o=o, q=q, hotb=hotb, at=at):
                cols = pl.ds(pl.multiple_of(j * tile, tile), tile)
                R[at, cols] = jnp.dot(
                    hotb, TOK[o, q, :, cols], preferred_element_type=F32
                ).astype(BF16)
                return 0

            lax.fori_loop(0, width // tile, gather, 0)
        span = pl.ds(base, cap * len(blocks))
        pre = jnp.dot(R[span, :], WC[...], preferred_element_type=F32)
        return picks, pre

    def cot_part(blocks, base, picks, pre, leave):
        for i, (o, q) in enumerate(blocks):
            at = pl.ds(base + i * cap, cap)

            def gather(j, _, o=o, q=q, hotb=picks[i][0], gsel=picks[i][1], at=at):
                cols = pl.ds(pl.multiple_of(j * tile, tile), tile)
                S[at, cols] = (
                    gsel * jnp.dot(hotb, COT[o, q, :, cols], preferred_element_type=F32)
                ).astype(BF16)
                return 0

            lax.fori_loop(0, width // tile, gather, 0)
        span = pl.ds(base, cap * len(blocks))
        back = lax.dot_general(S[span, :], WD[...], over_last, preferred_element_type=F32)
        gate_pre = pre[:, :hid]
        up_pre = pre[:, hid:]
        sigma = jax.nn.sigmoid(gate_pre)
        active = gate_pre * sigma
        H[span, :] = (active * up_pre).astype(BF16)
        GGU[span, pl.ds(0, hid)] = (
            back * up_pre * sigma * (1.0 + gate_pre * (1.0 - sigma))
        ).astype(BF16)
        GGU[span, pl.ds(hid, hid)] = (back * active).astype(BF16)

        def spread(j, _):
            cols = pl.ds(pl.multiple_of(j * tile, tile), tile)
            grads = lax.dot_general(
                GGU[span, :], WC[cols, :], over_last, preferred_element_type=F32
            ).astype(BF16)
            for i, (o, q) in enumerate(blocks):
                PART[o, q, :, cols] = jnp.dot(
                    picks[i][2], grads[i * cap : (i + 1) * cap], preferred_element_type=F32
                ).astype(BF16)
            return 0

        for w in (0, 1):
            lax.fori_loop(2 * w, 2 * w + 2, spread, 0)
            leave(w)

    def part_put(o, w):
        cols = pl.ds(w * (width // 2), width // 2)
        put(
            PART.at[o, 1, :, cols], SIB.at[o, :, cols], ps_send.at[o, w], ps_recv.at[o, w], sib
        )

    def part_take(o):
        for w in (0, 1):
            cols = pl.ds(w * (width // 2), width // 2)
            arrived(SIB.at[o, :, cols], ps_send.at[o, w], ps_recv.at[o, w], sib)

    def sib_takes(arrays, s):
        for a in arrays:
            if s == 0:
                arrived(bufs[a].at[0, 1], sib_send.at[a, 0], sib_recv.at[a, 0], sib)
            else:
                for d in (0, 1):
                    sib_take(a, d, s)

    def blocks_of(s):
        if s == 0:
            return (0,), 0
        return ((n - s, s) if s < half else (half,)), 2 * cap + (s - 1) * 4 * cap

    def tokens_of(s):
        sib_takes((2, 3, 0), s)
        offs, base = blocks_of(s)
        return token_part([(o, q) for o in offs for q in (0, 1)], base)

    def rest_of(s, picks, pre):
        sib_takes((1,), s)
        offs, base = blocks_of(s)

        def leave(w):
            for o in offs:
                part_put(o, w)

        cot_part([(o, q) for o in offs for q in (0, 1)], base, picks, pre, leave)

    def batch(s):
        if s == 0:
            for cp in local + weights:
                cp.wait()
        rest_of(s, *tokens_of(s))

    for s in range(1, half):
        for a in (2, 3, 0):
            for d in (0, 1):
                ring_take(a, d, s)
        batch(s - 1)
        for d in (0, 1):
            ring_take(1, d, s)
    batch(half - 1)
    for a in (2, 3, 0):
        for d in (0, 1):
            ring_take(a, d, half)
    def rs_dst(d, j, h):
        return RB.at[d, j - 1, pl.ds(h * qr, qr), :]

    def rs_send_piece(d, j, h):
        k = half - j + 1
        o = k if d == 0 else n - k
        add = j > 2 or (j == 2 and h // 2 == d)
        if add:
            arrived(rs_dst(d, j - 1, h), rs_send.at[d, j - 2, h], rs_recv.at[d, j - 2, h], nxt[d])

        def add_rows(i, _):
            r = pl.ds(pl.multiple_of(h * qr + i * 16, 16), 16)
            total = PART[o, 0, r, :].astype(F32) + SIB[o, r, :].astype(F32)
            if add:
                total = total + RB[d, j - 2, r, :].astype(F32)
            PART[o, 0, r, :] = total.astype(BF16)
            return 0

        lax.fori_loop(0, qr // 16, add_rows, 0)
        put(
            PART.at[o, 0, pl.ds(h * qr, qr), :], rs_dst(d, j, h),
            rs_send.at[d, j - 1, h], rs_recv.at[d, j - 1, h], nxt[d],
        )

    def early(j):
        for h in (0, 1):
            for d in (0, 1):
                rs_send_piece(d, j, 2 * (1 - d) + h)

    def late(j):
        for h in (0, 1):
            for d in (0, 1):
                rs_send_piece(d, j, 2 * d + h)

    def down_grad():
        def body(j, _):
            cols = pl.ds(pl.multiple_of(j * tile, tile), tile)
            out_down[0, :, cols] = lax.dot_general(
                H[...], S[:, cols], over_rows, preferred_element_type=F32
            ).astype(BF16)
            return 0

        lax.fori_loop(0, width // tile, body, 0)

    wt = width // 8

    def in_grads(lo, hi):
        def body(j, _):
            cols = pl.ds(pl.multiple_of(j * wt, wt), wt)
            both = lax.dot_general(R[:, cols], GGU[...], over_rows, preferred_element_type=F32)
            out_gate[0, cols, :] = both[:, :hid].astype(BF16)
            out_up[0, cols, :] = both[:, hid:].astype(BF16)
            return 0

        lax.fori_loop(lo, hi, body, 0)

    for o in range(n):
        if o not in (0, half):
            part_take(o)
    early(2)
    last = tokens_of(half)
    for d in (0, 1):
        ring_take(1, d, half)
    rest_of(half, *last)
    early(3)
    part_take(half)
    late(1)
    down_grad()
    in_grads(0, 1)
    for j in range(2, half + 1):
        late(j)
        if j + 2 <= half:
            early(j + 2)
        lo = 1 + 7 * (j - 2) // (half - 1)
        in_grads(lo, 1 + 7 * (j - 1) // (half - 1))
    part_take(0)

    def landed(d, h):
        arrived(
            rs_dst(d, half, h), rs_send.at[d, half - 1, h], rs_recv.at[d, half - 1, h], nxt[d]
        )

    for d in (0, 1):
        for h in (0, 1):
            landed(d, 2 * (1 - d) + h)
    for h in (0, 1):
        for d in (0, 1):
            landed(d, 2 * d + h)

            def final(i, _, d=d, h=h):
                r = pl.ds(pl.multiple_of((2 * d + h) * qr + i * 16, 16), 16)
                total = PART[0, 0, r, :].astype(F32) + SIB[0, r, :].astype(F32)
                total = total + RB[0, half - 1, r, :].astype(F32)
                total = total + RB[1, half - 1, r, :].astype(F32)
                out_tok[r, :] = total.astype(BF16)
                return 0

            lax.fori_loop(0, qr // 16, final, 0)
    for cp in sends:
        cp.wait_send()


def gathered(tokens, cotangent, routes, gates, helper, w_gate, w_up, w_down):
    rows, width = tokens.shape
    n = lax.axis_size("expert")
    devices = n * lax.axis_size("dp")
    hid = w_gate.shape[2]
    cap = 2 * rows * routes.shape[1] // devices
    home = cap - 3 * cap // 8
    half = n // 2
    slots = devices * cap
    top = routes.shape[1]
    anyw = pl.BlockSpec(memory_space=pl.ANY)
    vmem = pl.BlockSpec(memory_space=pltpu.VMEM)
    dma = pltpu.SemaphoreType.DMA
    return pl.pallas_call(
        functools.partial(ring_kernel, n, cap, home),
        out_shape=(
            pltpu.VMEM((rows, width), BF16),
            pltpu.VMEM((1, width, hid), BF16),
            pltpu.VMEM((1, width, hid), BF16),
            pltpu.VMEM((1, hid, width), BF16),
        ),
        in_specs=[anyw] * 8,
        out_specs=(vmem, vmem, vmem, vmem),
        scratch_shapes=[
            pltpu.VMEM((n, 2, rows, width), BF16),
            pltpu.VMEM((n, 2, rows, width), BF16),
            pltpu.VMEM((n, 2, top, rows), jnp.int32),
            pltpu.VMEM((n, 2, top, rows), F32),
            pltpu.VMEM((1, devices), jnp.int32),
            pltpu.VMEM((width, 2 * hid), BF16),
            pltpu.VMEM((hid, width), BF16),
            pltpu.VMEM((slots, width), BF16),
            pltpu.VMEM((slots, width), BF16),
            pltpu.VMEM((slots, hid), BF16),
            pltpu.VMEM((slots, 2 * hid), BF16),
            pltpu.VMEM((n, 2, rows, width), BF16),
            pltpu.VMEM((n, rows, width), BF16),
            pltpu.VMEM((2, half, rows, width), BF16),
            dma((5,)),
            dma((3,)),
            dma((4, 2, half)),
            dma((4, 2, half)),
            dma((4, 2 * half + 1)),
            dma((4, 2 * half + 1)),
            dma((n, 2)),
            dma((n, 2)),
            dma((2, half, 4)),
            dma((2, half, 4)),
        ],
        compiler_params=pltpu.CompilerParams(
            collective_id=0, has_side_effects=True, vmem_limit_bytes=56 * 1024 * 1024
        ),
    )(tokens, cotangent, routes.T, gates.T, helper[None], w_gate[0], w_up[0], w_down[0])


def flush_kernel(*refs):
    count = len(refs) // 2
    sems = refs[-1]
    copies = [
        pltpu.make_async_copy(refs[i], refs[count + i], sems.at[i]) for i in range(count)
    ]
    for cp in copies:
        cp.start()
    for cp in copies:
        cp.wait()


def flush(*arrays):
    return pl.pallas_call(
        flush_kernel,
        out_shape=tuple(jax.ShapeDtypeStruct(a.shape, a.dtype) for a in arrays),
        in_specs=[pl.BlockSpec(memory_space=pltpu.VMEM)] * len(arrays),
        out_specs=tuple(pl.BlockSpec(memory_space=pl.ANY) for _ in arrays),
        scratch_shapes=[pltpu.SemaphoreType.DMA((len(arrays),))],
        compiler_params=pltpu.CompilerParams(vmem_limit_bytes=1024 * 1024),
    )(*arrays)


def plan(tokens, cotangent, routes, *rest):
    rows = tokens.shape[0]
    n, cores = lax.axis_size("expert"), lax.axis_size("dp")
    slots = 2 * rows * routes.shape[1]
    few = cores == 2 and n % 2 == 0 and n >= 6 and rows % 64 == 0 and n * cores * rows <= 2 * slots
    if few:
        return flush(*gathered(tokens, cotangent, routes, *rest))
    return local(tokens, cotangent, routes, *rest)


def solution(mesh):
    return jax.shard_map(
        plan,
        mesh=mesh,
        in_specs=(
            P(("groups", "expert", "dp"), None),
            P(("groups", "expert", "dp"), None),
            P(("groups", "expert", "dp"), None),
            P(("groups", "expert", "dp"), None),
            P("groups"),
            P(("expert", "dp"), None, None),
            P(("expert", "dp"), None, None),
            P(("expert", "dp"), None, None),
        ),
        out_specs=(
            P(("groups", "expert", "dp"), None),
            P(("groups", "expert", "dp"), None, None),
            P(("groups", "expert", "dp"), None, None),
            P(("groups", "expert", "dp"), None, None),
        ),
        check_vma=False,
    )
```

```python
import functools

import jax
import jax.numpy as jnp
from jax import lax
from jax.experimental import pallas as pl
from jax.experimental.pallas import tpu as pltpu
from jax.sharding import PartitionSpec as P

MESH = pl.DeviceIdType.MESH
BF16 = jnp.bfloat16
F32 = jnp.float32


def expert_pass(rows, scaled, gate_w, up_w, down_w):
    gate_pre = jnp.dot(rows, gate_w, preferred_element_type=jnp.float32)
    up_pre = jnp.dot(rows, up_w, preferred_element_type=jnp.float32)
    sigma = jax.nn.sigmoid(gate_pre)
    active = gate_pre * sigma
    hidden = (active * up_pre).astype(jnp.bfloat16)
    over_last = (((1,), (1,)), ((), ()))
    over_rows = (((0,), (0,)), ((), ()))
    back_hidden = lax.dot_general(scaled, down_w, over_last, preferred_element_type=jnp.float32)
    grad_gating = (back_hidden * up_pre * sigma * (1.0 + gate_pre * (1.0 - sigma))).astype(
        jnp.bfloat16
    )
    grad_upward = (back_hidden * active).astype(jnp.bfloat16)
    grad_down = lax.dot_general(hidden, scaled, over_rows, preferred_element_type=jnp.float32)
    grad_gate = lax.dot_general(rows, grad_gating, over_rows, preferred_element_type=jnp.float32)
    grad_up = lax.dot_general(rows, grad_upward, over_rows, preferred_element_type=jnp.float32)
    row_grads = lax.dot_general(grad_gating, gate_w, over_last, preferred_element_type=jnp.float32)
    row_grads = row_grads + lax.dot_general(
        grad_upward, up_w, over_last, preferred_element_type=jnp.float32
    )
    return (row_grads.astype(jnp.bfloat16), grad_gate, grad_up, grad_down)


def local(tokens, cotangent, routes, gates, helper, w_gate, w_up, w_down):
    tok_rows, width = tokens.shape
    top_count = routes.shape[1]
    devices = lax.axis_size(("expert", "dp"))
    route_cap = 2 * tok_rows * top_count // devices
    spill_cap = 3 * route_cap // 8
    home_cap = route_cap - spill_cap
    block_rows = tok_rows * top_count
    slots = devices * route_cap
    flat_ids = routes.reshape(block_rows)
    experts_row = jnp.arange(devices, dtype=jnp.int32)
    one_hot = (flat_ids[:, None] == experts_row[None, :]).astype(jnp.float32)
    positions = jnp.arange(block_rows, dtype=jnp.int32)
    lower = (positions[:, None] > positions[None, :]).astype(jnp.float32)
    before = jnp.dot(lower, one_hot, precision=lax.Precision.HIGHEST)
    route_rank = jnp.sum(before * one_hot, axis=1).astype(jnp.int32)
    partner_help = helper.reshape(devices // 2, 2)[:, ::-1].reshape(devices).astype(jnp.float32)
    helped = jnp.dot(one_hot, partner_help, precision=lax.Precision.HIGHEST) > 0.5
    spilled = route_rank >= home_cap
    kept = jnp.logical_not(spilled) | helped
    slot_index = jnp.where(kept, flat_ids * route_cap + route_rank, slots)
    source = jnp.full((slots + 1,), block_rows, jnp.int32).at[slot_index].set(positions)[:slots]
    token_of = jnp.where(source < block_rows, source // top_count, tok_rows)
    tokens_pad = jnp.concatenate([tokens, jnp.zeros((1, width), jnp.bfloat16)], axis=0)
    cot_pad = jnp.concatenate([cotangent, jnp.zeros((1, width), jnp.bfloat16)], axis=0)
    gate_pad = jnp.concatenate([gates.reshape(block_rows), jnp.zeros((1,), jnp.float32)], axis=0)
    send_rows = tokens_pad[token_of].reshape(devices, route_cap, width)
    send_scaled = (cot_pad[token_of].astype(jnp.float32) * gate_pad[source][:, None]).astype(
        jnp.bfloat16
    )
    send_scaled = send_scaled.reshape(devices, route_cap, width)
    recv_rows, recv_scaled = (
        lax.all_to_all(send_rows, ("expert", "dp"), split_axis=0, concat_axis=0, tiled=True),
        lax.all_to_all(send_scaled, ("expert", "dp"), split_axis=0, concat_axis=0, tiled=True),
    )
    gate_w = w_gate[0]
    up_w = w_up[0]
    down_w = w_down[0]
    whole_out = expert_pass(
        recv_rows.reshape(slots, width), recv_scaled.reshape(slots, width), gate_w, up_w, down_w
    )
    grad_gate = whole_out[1]
    grad_up = whole_out[2]
    grad_down = whole_out[3]
    row_grads = whole_out[0].reshape(devices, route_cap, width)
    back_rows = lax.all_to_all(row_grads, ("expert", "dp"), split_axis=0, concat_axis=0, tiled=True)
    back_pad = jnp.concatenate(
        [back_rows.reshape(slots, width), jnp.zeros((1, width), jnp.bfloat16)], axis=0
    )
    picked = back_pad[slot_index].reshape(tok_rows, top_count, width)
    grad_tokens = jnp.sum(picked.astype(jnp.float32), axis=1).astype(jnp.bfloat16)
    return (
        grad_tokens,
        grad_gate[None].astype(jnp.bfloat16),
        grad_up[None].astype(jnp.bfloat16),
        grad_down[None].astype(jnp.bfloat16),
    )


def ring_kernel(
    n, cap, home,
    tok_in, cot_in, rt_in, gt_in, help_in, wg_in, wu_in, wd_in,
    out_tok, out_gate, out_up, out_down,
    TOK, COT, RT, GT, HELP, WC, WD, R, S, H, GGU, PART, SIB, RB,
    lsem, wsem, ag_send, ag_recv, sib_send, sib_recv,
    ps_send, ps_recv, rs_send, rs_recv,
):
    half = n // 2
    rows, width = tok_in.shape
    hid = wd_in.shape[0]
    hr = rows // 2
    hw = width // 2
    tile = width // 4
    e = lax.axis_index("expert")
    c = lax.axis_index("dp")
    z = e // 2
    x = e % 2
    pos = z + x * (n - 1 - 2 * z)

    def chip_at(q):
        q = q % n
        side = q // half
        return side * (2 * (n - 1 - q) + 1) + (1 - side) * 2 * q

    nxt = ({"expert": chip_at(pos + 1)}, {"expert": chip_at(pos + n - 1)})
    sib = {"dp": 1 - c}
    me = e * 2 + c

    def far(d):
        return pl.ds(d * hr, hr)

    local = [
        pltpu.make_async_copy(tok_in, TOK.at[0, 0], lsem.at[0]),
        pltpu.make_async_copy(cot_in, COT.at[0, 0], lsem.at[1]),
        pltpu.make_async_copy(rt_in, RT.at[0, 0], lsem.at[2]),
        pltpu.make_async_copy(gt_in, GT.at[0, 0], lsem.at[3]),
        pltpu.make_async_copy(help_in, HELP, lsem.at[4]),
    ]
    weights = [
        pltpu.make_async_copy(wg_in, WC.at[:, pl.ds(0, hid)], wsem.at[0]),
        pltpu.make_async_copy(wu_in, WC.at[:, pl.ds(hid, hid)], wsem.at[1]),
        pltpu.make_async_copy(wd_in, WD, wsem.at[2]),
    ]
    for cp in local + weights:
        cp.start()

    barrier = pltpu.get_barrier_semaphore()
    for who in (nxt[0], nxt[1], sib):
        pl.semaphore_signal(barrier, inc=1, device_id=who, device_id_type=MESH)
    pl.semaphore_wait(barrier, 3)

    bufs = (TOK, COT, RT, GT)
    own = (tok_in, cot_in, rt_in, gt_in)
    order = (2, 3, 0, 1)
    sends = []

    def put(src, dst, ssem, rsem, who):
        cp = pltpu.make_async_remote_copy(
            src_ref=src, dst_ref=dst, send_sem=ssem, recv_sem=rsem,
            device_id=who, device_id_type=MESH,
        )
        cp.start()
        sends.append(cp)

    def arrived(dst, ssem, rsem, who):
        pltpu.make_async_remote_copy(
            src_ref=dst, dst_ref=dst, send_sem=ssem, recv_sem=rsem,
            device_id=who, device_id_type=MESH,
        ).wait_recv()

    def slot(d, s):
        return (n - s) % n if d == 0 else s % n

    def piece(a, d, s):
        ref = bufs[a].at[slot(d, s), 0]
        if s == half and a < 2:
            return ref.at[far(d), :]
        return ref

    def sib_piece(a, d, s):
        ref = bufs[a].at[slot(d, s), 1]
        if s == half and a < 2:
            return ref.at[far(d), :]
        return ref

    def ring_put(a, d, s):
        if s == half and a >= 2 and d == 1:
            return
        src = own[a] if s == 1 else bufs[a].at[slot(d, s - 1), 0]
        if s == half and a < 2:
            src = src.at[far(d), :]
        put(src, piece(a, d, s), ag_send.at[a, d, s - 1], ag_recv.at[a, d, s - 1], nxt[d])

    def ring_take(a, d, s):
        if s == half and a >= 2 and d == 1:
            return
        arrived(piece(a, d, s), ag_send.at[a, d, s - 1], ag_recv.at[a, d, s - 1], nxt[d])
        if s < half:
            ring_put(a, d, s + 1)
        k = 1 + d * half + s - 1
        put(piece(a, d, s), sib_piece(a, d, s), sib_send.at[a, k], sib_recv.at[a, k], sib)

    def sib_take(a, d, s):
        if s == half and a >= 2 and d == 1:
            return
        k = 1 + d * half + s - 1
        arrived(sib_piece(a, d, s), sib_send.at[a, k], sib_recv.at[a, k], sib)

    for a in order:
        for d in (0, 1):
            ring_put(a, d, 1)
    for a in order:
        put(own[a], bufs[a].at[0, 1], sib_send.at[a, 0], sib_recv.at[a, 0], sib)

    earlier = (
        lax.broadcasted_iota(jnp.int32, (rows, rows), 0)
        < lax.broadcasted_iota(jnp.int32, (rows, rows), 1)
    ).astype(BF16)
    slot_ids = lax.broadcasted_iota(jnp.int32, (cap, rows), 0).astype(F32)
    over_last = (((1,), (1,)), ((), ()))
    over_rows = (((0,), (0,)), ((), ()))

    def token_part(blocks, base):
        partner = me + 1 - 2 * (me % 2)
        lanes = lax.broadcasted_iota(jnp.int32, HELP.shape, 1)
        flag = jnp.sum(jnp.where(lanes == partner, HELP[...], 0).astype(F32), axis=1, keepdims=True)
        limit = jnp.where(flag == 1.0, float(rows), home - 0.5)
        picks = []
        for i, (o, q) in enumerate(blocks):
            hit = RT[o, q] == me
            named = jnp.sum(hit.astype(F32), axis=0, keepdims=True)
            gate = jnp.sum(jnp.where(hit, GT[o, q], 0.0), axis=0, keepdims=True)
            named16 = jnp.broadcast_to(named, (16, rows)).astype(BF16)
            rank = jnp.dot(named16, earlier, preferred_element_type=F32)[0:1]
            kept = (named > 0.5) & (rank < limit)
            place = jnp.where(kept, rank, -1.0)
            hot = slot_ids == place
            gsel = jnp.sum(jnp.where(hot, gate, 0.0), axis=1, keepdims=True)
            hotf = hot.astype(F32)
            hotb = hotf.astype(BF16)
            picks.append((hotb, gsel, jnp.transpose(hotf).astype(BF16)))
            at = pl.ds(base + i * cap, cap)

            def gather(j, _, o=o, q=q, hotb=hotb, at=at):
                cols = pl.ds(pl.multiple_of(j * tile, tile), tile)
                R[at, cols] = jnp.dot(
                    hotb, TOK[o, q, :, cols], preferred_element_type=F32
                ).astype(BF16)
                return 0

            lax.fori_loop(0, width // tile, gather, 0)
        span = pl.ds(base, cap * len(blocks))
        pre = jnp.dot(R[span, :], WC[...], preferred_element_type=F32)
        return picks, pre

    def cot_part(blocks, base, picks, pre, leave):
        for i, (o, q) in enumerate(blocks):
            at = pl.ds(base + i * cap, cap)

            def gather(j, _, o=o, q=q, hotb=picks[i][0], gsel=picks[i][1], at=at):
                cols = pl.ds(pl.multiple_of(j * tile, tile), tile)
                S[at, cols] = (
                    gsel * jnp.dot(hotb, COT[o, q, :, cols], preferred_element_type=F32)
                ).astype(BF16)
                return 0

            lax.fori_loop(0, width // tile, gather, 0)
        span = pl.ds(base, cap * len(blocks))
        back = lax.dot_general(S[span, :], WD[...], over_last, preferred_element_type=F32)
        gate_pre = pre[:, :hid]
        up_pre = pre[:, hid:]
        sigma = jax.nn.sigmoid(gate_pre)
        active = gate_pre * sigma
        H[span, :] = (active * up_pre).astype(BF16)
        GGU[span, pl.ds(0, hid)] = (
            back * up_pre * sigma * (1.0 + gate_pre * (1.0 - sigma))
        ).astype(BF16)
        GGU[span, pl.ds(hid, hid)] = (back * active).astype(BF16)

        def spread(j, _):
            cols = pl.ds(pl.multiple_of(j * tile, tile), tile)
            grads = lax.dot_general(
                GGU[span, :], WC[cols, :], over_last, preferred_element_type=F32
            ).astype(BF16)
            for i, (o, q) in enumerate(blocks):
                PART[o, q, :, cols] = jnp.dot(
                    picks[i][2], grads[i * cap : (i + 1) * cap], preferred_element_type=F32
                ).astype(BF16)
            return 0

        for w in (0, 1):
            lax.fori_loop(2 * w, 2 * w + 2, spread, 0)
            leave(w)

    def part_put(o, w):
        cols = pl.ds(w * (width // 2), width // 2)
        put(
            PART.at[o, 1, :, cols], SIB.at[o, :, cols], ps_send.at[o, w], ps_recv.at[o, w], sib
        )

    def part_take(o, halves=(0, 1)):
        for w in halves:
            cols = pl.ds(w * (width // 2), width // 2)
            arrived(SIB.at[o, :, cols], ps_send.at[o, w], ps_recv.at[o, w], sib)

    def sib_takes(arrays, s):
        for a in arrays:
            if s == 0:
                arrived(bufs[a].at[0, 1], sib_send.at[a, 0], sib_recv.at[a, 0], sib)
            else:
                for d in (0, 1):
                    sib_take(a, d, s)

    def blocks_of(s):
        if s == 0:
            return (0,), 0
        return ((n - s, s) if s < half else (half,)), 2 * cap + (s - 1) * 4 * cap

    def tokens_of(s):
        sib_takes((2, 3, 0), s)
        offs, base = blocks_of(s)
        return token_part([(o, q) for o in offs for q in (0, 1)], base)

    def rest_of(s, picks, pre):
        sib_takes((1,), s)
        offs, base = blocks_of(s)

        def leave(w):
            for o in offs:
                part_put(o, w)

        cot_part([(o, q) for o in offs for q in (0, 1)], base, picks, pre, leave)

    def batch(s):
        if s == 0:
            for cp in local + weights:
                cp.wait()
        rest_of(s, *tokens_of(s))

    for cp in local + weights:
        cp.wait()
    rest_of(0, *tokens_of(0))
    for s in range(1, half):
        for a in (2, 3, 0):
            for d in (0, 1):
                ring_take(a, d, s)
        ready = tokens_of(s)
        for d in (0, 1):
            ring_take(1, d, s)
        rest_of(s, *ready)
    for a in (2, 3, 0):
        for d in (0, 1):
            ring_take(a, d, half)

    def rs_dst(d, j, h):
        return RB.at[d, j - 1, pl.ds(h // 2 * hr, hr), pl.ds(h % 2 * hw, hw)]

    def rs_send_piece(d, j, h):
        k = half - j + 1
        o = k if d == 0 else n - k
        add = j > 2 or (j == 2 and h // 2 == d)
        if add:
            arrived(rs_dst(d, j - 1, h), rs_send.at[d, j - 2, h], rs_recv.at[d, j - 2, h], nxt[d])

        cols = pl.ds(h % 2 * hw, hw)

        def add_rows(i, _):
            r = pl.ds(pl.multiple_of(h // 2 * hr + i * 16, 16), 16)
            total = PART[o, 0, r, cols].astype(F32) + SIB[o, r, cols].astype(F32)
            if add:
                total = total + RB[d, j - 2, r, cols].astype(F32)
            PART[o, 0, r, cols] = total.astype(BF16)
            return 0

        lax.fori_loop(0, hr // 16, add_rows, 0)
        put(
            PART.at[o, 0, pl.ds(h // 2 * hr, hr), cols], rs_dst(d, j, h),
            rs_send.at[d, j - 1, h], rs_recv.at[d, j - 1, h], nxt[d],
        )

    def early(j):
        for h in (0, 1):
            for d in (0, 1):
                rs_send_piece(d, j, 2 * (1 - d) + h)

    def late(j):
        for h in (0, 1):
            for d in (0, 1):
                rs_send_piece(d, j, 2 * d + h)

    def down_grad():
        def body(j, _):
            cols = pl.ds(pl.multiple_of(j * tile, tile), tile)
            out_down[0, :, cols] = lax.dot_general(
                H[...], S[:, cols], over_rows, preferred_element_type=F32
            ).astype(BF16)
            return 0

        lax.fori_loop(0, width // tile, body, 0)

    wt = width // 8

    def in_grads(lo, hi):
        def body(j, _):
            cols = pl.ds(pl.multiple_of(j * wt, wt), wt)
            both = lax.dot_general(R[:, cols], GGU[...], over_rows, preferred_element_type=F32)
            out_gate[0, cols, :] = both[:, :hid].astype(BF16)
            out_up[0, cols, :] = both[:, hid:].astype(BF16)
            return 0

        lax.fori_loop(lo, hi, body, 0)

    for o in range(n):
        if o not in (0, half):
            part_take(o)
    early(2)
    last = tokens_of(half)
    for d in (0, 1):
        ring_take(1, d, half)
    rest_of(half, *last)
    early(3)
    for h in (0, 1):
        part_take(half, (h,))
        for d in (0, 1):
            rs_send_piece(d, 1, 2 * d + h)
    down_grad()
    in_grads(0, 1)
    for j in range(2, half + 1):
        late(j)
        if j + 2 <= half:
            early(j + 2)
        lo = 1 + 7 * (j - 2) // (half - 1)
        in_grads(lo, 1 + 7 * (j - 1) // (half - 1))
    part_take(0)

    def landed(d, h):
        arrived(
            rs_dst(d, half, h), rs_send.at[d, half - 1, h], rs_recv.at[d, half - 1, h], nxt[d]
        )

    for d in (0, 1):
        for h in (0, 1):
            landed(d, 2 * (1 - d) + h)
    for h in (0, 1):
        for d in (0, 1):
            landed(d, 2 * d + h)

            def final(i, _, d=d, h=h):
                cols = pl.ds(h * hw, hw)
                r = pl.ds(pl.multiple_of(d * hr + i * 16, 16), 16)
                total = PART[0, 0, r, cols].astype(F32) + SIB[0, r, cols].astype(F32)
                total = total + RB[0, half - 1, r, cols].astype(F32)
                total = total + RB[1, half - 1, r, cols].astype(F32)
                out_tok[r, cols] = total.astype(BF16)
                return 0

            lax.fori_loop(0, hr // 16, final, 0)
    for cp in sends:
        cp.wait_send()


def gathered(tokens, cotangent, routes, gates, helper, w_gate, w_up, w_down):
    rows, width = tokens.shape
    n = lax.axis_size("expert")
    devices = n * lax.axis_size("dp")
    hid = w_gate.shape[2]
    cap = 2 * rows * routes.shape[1] // devices
    home = cap - 3 * cap // 8
    half = n // 2
    slots = devices * cap
    top = routes.shape[1]
    anyw = pl.BlockSpec(memory_space=pl.ANY)
    vmem = pl.BlockSpec(memory_space=pltpu.VMEM)
    dma = pltpu.SemaphoreType.DMA
    return pl.pallas_call(
        functools.partial(ring_kernel, n, cap, home),
        out_shape=(
            pltpu.VMEM((rows, width), BF16),
            pltpu.VMEM((1, width, hid), BF16),
            pltpu.VMEM((1, width, hid), BF16),
            pltpu.VMEM((1, hid, width), BF16),
        ),
        in_specs=[anyw] * 8,
        out_specs=(vmem, vmem, vmem, vmem),
        scratch_shapes=[
            pltpu.VMEM((n, 2, rows, width), BF16),
            pltpu.VMEM((n, 2, rows, width), BF16),
            pltpu.VMEM((n, 2, top, rows), jnp.int32),
            pltpu.VMEM((n, 2, top, rows), F32),
            pltpu.VMEM((1, devices), jnp.int32),
            pltpu.VMEM((width, 2 * hid), BF16),
            pltpu.VMEM((hid, width), BF16),
            pltpu.VMEM((slots, width), BF16),
            pltpu.VMEM((slots, width), BF16),
            pltpu.VMEM((slots, hid), BF16),
            pltpu.VMEM((slots, 2 * hid), BF16),
            pltpu.VMEM((n, 2, rows, width), BF16),
            pltpu.VMEM((n, rows, width), BF16),
            pltpu.VMEM((2, half, rows, width), BF16),
            dma((5,)),
            dma((3,)),
            dma((4, 2, half)),
            dma((4, 2, half)),
            dma((4, 2 * half + 1)),
            dma((4, 2 * half + 1)),
            dma((n, 2)),
            dma((n, 2)),
            dma((2, half, 4)),
            dma((2, half, 4)),
        ],
        compiler_params=pltpu.CompilerParams(
            collective_id=0, has_side_effects=True, vmem_limit_bytes=56 * 1024 * 1024
        ),
    )(tokens, cotangent, routes.T, gates.T, helper[None], w_gate[0], w_up[0], w_down[0])


def flush_kernel(*refs):
    count = len(refs) // 2
    sems = refs[-1]
    copies = []
    for i in range(count):
        rows = refs[i].shape[-2]
        parts = 4 if rows % 64 == 0 else 1
        for k in range(parts):
            at = pl.ds(k * (rows // parts), rows // parts)
            at = (at,) if len(refs[i].shape) == 2 else (0, at)
            copies.append(
                pltpu.make_async_copy(refs[i].at[at], refs[count + i].at[at], sems.at[i, k])
            )
    for cp in copies:
        cp.start()
    for cp in copies:
        cp.wait()


def flush(*arrays):
    return pl.pallas_call(
        flush_kernel,
        out_shape=tuple(jax.ShapeDtypeStruct(a.shape, a.dtype) for a in arrays),
        in_specs=[pl.BlockSpec(memory_space=pltpu.VMEM)] * len(arrays),
        out_specs=tuple(pl.BlockSpec(memory_space=pl.ANY) for _ in arrays),
        scratch_shapes=[pltpu.SemaphoreType.DMA((len(arrays), 4))],
        compiler_params=pltpu.CompilerParams(vmem_limit_bytes=1024 * 1024),
    )(*arrays)


def plan(tokens, cotangent, routes, *rest):
    rows = tokens.shape[0]
    n, cores = lax.axis_size("expert"), lax.axis_size("dp")
    slots = 2 * rows * routes.shape[1]
    few = cores == 2 and n % 2 == 0 and n >= 6 and rows % 64 == 0 and n * cores * rows <= 2 * slots
    if few:
        return flush(*gathered(tokens, cotangent, routes, *rest))
    return local(tokens, cotangent, routes, *rest)


def solution(mesh):
    return jax.shard_map(
        plan,
        mesh=mesh,
        in_specs=(
            P(("groups", "expert", "dp"), None),
            P(("groups", "expert", "dp"), None),
            P(("groups", "expert", "dp"), None),
            P(("groups", "expert", "dp"), None),
            P("groups"),
            P(("expert", "dp"), None, None),
            P(("expert", "dp"), None, None),
            P(("expert", "dp"), None, None),
        ),
        out_specs=(
            P(("groups", "expert", "dp"), None),
            P(("groups", "expert", "dp"), None, None),
            P(("groups", "expert", "dp"), None, None),
            P(("groups", "expert", "dp"), None, None),
        ),
        check_vma=False,
    )
```

```python
import functools

import jax
import jax.numpy as jnp
from jax import lax
from jax.experimental import pallas as pl
from jax.experimental.pallas import tpu as pltpu
from jax.sharding import PartitionSpec as P

MESH = pl.DeviceIdType.MESH
BF16 = jnp.bfloat16
F32 = jnp.float32


def expert_pass(rows, scaled, gate_w, up_w, down_w):
    gate_pre = jnp.dot(rows, gate_w, preferred_element_type=jnp.float32)
    up_pre = jnp.dot(rows, up_w, preferred_element_type=jnp.float32)
    sigma = jax.nn.sigmoid(gate_pre)
    active = gate_pre * sigma
    hidden = (active * up_pre).astype(jnp.bfloat16)
    over_last = (((1,), (1,)), ((), ()))
    over_rows = (((0,), (0,)), ((), ()))
    back_hidden = lax.dot_general(scaled, down_w, over_last, preferred_element_type=jnp.float32)
    grad_gating = (back_hidden * up_pre * sigma * (1.0 + gate_pre * (1.0 - sigma))).astype(
        jnp.bfloat16
    )
    grad_upward = (back_hidden * active).astype(jnp.bfloat16)
    grad_down = lax.dot_general(hidden, scaled, over_rows, preferred_element_type=jnp.float32)
    grad_gate = lax.dot_general(rows, grad_gating, over_rows, preferred_element_type=jnp.float32)
    grad_up = lax.dot_general(rows, grad_upward, over_rows, preferred_element_type=jnp.float32)
    row_grads = lax.dot_general(grad_gating, gate_w, over_last, preferred_element_type=jnp.float32)
    row_grads = row_grads + lax.dot_general(
        grad_upward, up_w, over_last, preferred_element_type=jnp.float32
    )
    return (row_grads.astype(jnp.bfloat16), grad_gate, grad_up, grad_down)


def local(tokens, cotangent, routes, gates, helper, w_gate, w_up, w_down):
    tok_rows, width = tokens.shape
    top_count = routes.shape[1]
    devices = lax.axis_size(("expert", "dp"))
    route_cap = 2 * tok_rows * top_count // devices
    spill_cap = 3 * route_cap // 8
    home_cap = route_cap - spill_cap
    block_rows = tok_rows * top_count
    slots = devices * route_cap
    flat_ids = routes.reshape(block_rows)
    experts_row = jnp.arange(devices, dtype=jnp.int32)
    one_hot = (flat_ids[:, None] == experts_row[None, :]).astype(jnp.float32)
    positions = jnp.arange(block_rows, dtype=jnp.int32)
    lower = (positions[:, None] > positions[None, :]).astype(jnp.float32)
    before = jnp.dot(lower, one_hot, precision=lax.Precision.HIGHEST)
    route_rank = jnp.sum(before * one_hot, axis=1).astype(jnp.int32)
    partner_help = helper.reshape(devices // 2, 2)[:, ::-1].reshape(devices).astype(jnp.float32)
    helped = jnp.dot(one_hot, partner_help, precision=lax.Precision.HIGHEST) > 0.5
    spilled = route_rank >= home_cap
    kept = jnp.logical_not(spilled) | helped
    slot_index = jnp.where(kept, flat_ids * route_cap + route_rank, slots)
    source = jnp.full((slots + 1,), block_rows, jnp.int32).at[slot_index].set(positions)[:slots]
    token_of = jnp.where(source < block_rows, source // top_count, tok_rows)
    tokens_pad = jnp.concatenate([tokens, jnp.zeros((1, width), jnp.bfloat16)], axis=0)
    cot_pad = jnp.concatenate([cotangent, jnp.zeros((1, width), jnp.bfloat16)], axis=0)
    gate_pad = jnp.concatenate([gates.reshape(block_rows), jnp.zeros((1,), jnp.float32)], axis=0)
    send_rows = tokens_pad[token_of].reshape(devices, route_cap, width)
    send_scaled = (cot_pad[token_of].astype(jnp.float32) * gate_pad[source][:, None]).astype(
        jnp.bfloat16
    )
    send_scaled = send_scaled.reshape(devices, route_cap, width)
    recv_rows, recv_scaled = (
        lax.all_to_all(send_rows, ("expert", "dp"), split_axis=0, concat_axis=0, tiled=True),
        lax.all_to_all(send_scaled, ("expert", "dp"), split_axis=0, concat_axis=0, tiled=True),
    )
    gate_w = w_gate[0]
    up_w = w_up[0]
    down_w = w_down[0]
    whole_out = expert_pass(
        recv_rows.reshape(slots, width), recv_scaled.reshape(slots, width), gate_w, up_w, down_w
    )
    grad_gate = whole_out[1]
    grad_up = whole_out[2]
    grad_down = whole_out[3]
    row_grads = whole_out[0].reshape(devices, route_cap, width)
    back_rows = lax.all_to_all(row_grads, ("expert", "dp"), split_axis=0, concat_axis=0, tiled=True)
    back_pad = jnp.concatenate(
        [back_rows.reshape(slots, width), jnp.zeros((1, width), jnp.bfloat16)], axis=0
    )
    picked = back_pad[slot_index].reshape(tok_rows, top_count, width)
    grad_tokens = jnp.sum(picked.astype(jnp.float32), axis=1).astype(jnp.bfloat16)
    return (
        grad_tokens,
        grad_gate[None].astype(jnp.bfloat16),
        grad_up[None].astype(jnp.bfloat16),
        grad_down[None].astype(jnp.bfloat16),
    )


def ring_kernel(
    n, cap, home,
    tok_in, cot_in, rt_in, gt_in, help_in, wg_in, wu_in, wd_in,
    out_tok, out_gate, out_up, out_down,
    TOK, COT, RT, GT, HELP, WC, WD, R, S, H, GGU, PART, SIB, RB,
    lsem, wsem, ag_send, ag_recv, sib_send, sib_recv,
    ps_send, ps_recv, rs_send, rs_recv,
):
    half = n // 2
    rows, width = tok_in.shape
    hid = wd_in.shape[0]
    hr = rows // 2
    hw = width // 2
    tile = width // 4
    e = lax.axis_index("expert")
    c = lax.axis_index("dp")
    z = e // 2
    x = e % 2
    pos = z + x * (n - 1 - 2 * z)

    def chip_at(q):
        q = q % n
        side = q // half
        return side * (2 * (n - 1 - q) + 1) + (1 - side) * 2 * q

    nxt = ({"expert": chip_at(pos + 1)}, {"expert": chip_at(pos + n - 1)})
    sib = {"dp": 1 - c}
    me = e * 2 + c

    def far(d):
        return pl.ds(d * hr, hr)

    local = [
        pltpu.make_async_copy(tok_in, TOK.at[0, 0], lsem.at[0]),
        pltpu.make_async_copy(cot_in, COT.at[0, 0], lsem.at[1]),
        pltpu.make_async_copy(rt_in, RT.at[0, 0], lsem.at[2]),
        pltpu.make_async_copy(gt_in, GT.at[0, 0], lsem.at[3]),
        pltpu.make_async_copy(help_in, HELP, lsem.at[4]),
    ]
    weights = [
        pltpu.make_async_copy(wg_in, WC.at[:, pl.ds(0, hid)], wsem.at[0]),
        pltpu.make_async_copy(wu_in, WC.at[:, pl.ds(hid, hid)], wsem.at[1]),
        pltpu.make_async_copy(wd_in, WD, wsem.at[2]),
    ]
    for cp in local + weights:
        cp.start()

    barrier = pltpu.get_barrier_semaphore()
    for who in (nxt[0], nxt[1], sib):
        pl.semaphore_signal(barrier, inc=1, device_id=who, device_id_type=MESH)
    pl.semaphore_wait(barrier, 3)

    bufs = (TOK, COT, RT, GT)
    own = (tok_in, cot_in, rt_in, gt_in)
    order = (2, 3, 0, 1)
    sends = []

    def put(src, dst, ssem, rsem, who):
        cp = pltpu.make_async_remote_copy(
            src_ref=src, dst_ref=dst, send_sem=ssem, recv_sem=rsem,
            device_id=who, device_id_type=MESH,
        )
        cp.start()
        sends.append(cp)

    def arrived(dst, ssem, rsem, who):
        pltpu.make_async_remote_copy(
            src_ref=dst, dst_ref=dst, send_sem=ssem, recv_sem=rsem,
            device_id=who, device_id_type=MESH,
        ).wait_recv()

    def slot(d, s):
        return (n - s) % n if d == 0 else s % n

    def piece(a, d, s):
        ref = bufs[a].at[slot(d, s), 0]
        if s == half and a < 2:
            return ref.at[far(d), :]
        return ref

    def sib_piece(a, d, s):
        ref = bufs[a].at[slot(d, s), 1]
        if s == half and a < 2:
            return ref.at[far(d), :]
        return ref

    def ring_put(a, d, s):
        if s == half and a >= 2 and d == 1:
            return
        src = own[a] if s == 1 else bufs[a].at[slot(d, s - 1), 0]
        if s == half and a < 2:
            src = src.at[far(d), :]
        put(src, piece(a, d, s), ag_send.at[a, d, s - 1], ag_recv.at[a, d, s - 1], nxt[d])

    def ring_take(a, d, s):
        if s == half and a >= 2 and d == 1:
            return
        arrived(piece(a, d, s), ag_send.at[a, d, s - 1], ag_recv.at[a, d, s - 1], nxt[d])
        if s < half:
            ring_put(a, d, s + 1)
        k = 1 + d * half + s - 1
        put(piece(a, d, s), sib_piece(a, d, s), sib_send.at[a, k], sib_recv.at[a, k], sib)

    def sib_take(a, d, s):
        if s == half and a >= 2 and d == 1:
            return
        k = 1 + d * half + s - 1
        arrived(sib_piece(a, d, s), sib_send.at[a, k], sib_recv.at[a, k], sib)

    for a in order:
        for d in (0, 1):
            ring_put(a, d, 1)
    for a in order:
        put(own[a], bufs[a].at[0, 1], sib_send.at[a, 0], sib_recv.at[a, 0], sib)

    earlier = (
        lax.broadcasted_iota(jnp.int32, (rows, rows), 0)
        < lax.broadcasted_iota(jnp.int32, (rows, rows), 1)
    ).astype(BF16)
    slot_ids = lax.broadcasted_iota(jnp.int32, (cap, rows), 0).astype(F32)
    over_last = (((1,), (1,)), ((), ()))
    over_rows = (((0,), (0,)), ((), ()))

    def token_part(blocks, base):
        partner = me + 1 - 2 * (me % 2)
        lanes = lax.broadcasted_iota(jnp.int32, HELP.shape, 1)
        flag = jnp.sum(jnp.where(lanes == partner, HELP[...], 0).astype(F32), axis=1, keepdims=True)
        limit = jnp.where(flag == 1.0, float(rows), home - 0.5)
        picks = []
        for i, (o, q) in enumerate(blocks):
            hit = RT[o, q] == me
            named = jnp.sum(hit.astype(F32), axis=0, keepdims=True)
            gate = jnp.sum(jnp.where(hit, GT[o, q], 0.0), axis=0, keepdims=True)
            named16 = jnp.broadcast_to(named, (16, rows)).astype(BF16)
            rank = jnp.dot(named16, earlier, preferred_element_type=F32)[0:1]
            kept = (named > 0.5) & (rank < limit)
            place = jnp.where(kept, rank, -1.0)
            hot = slot_ids == place
            gsel = jnp.sum(jnp.where(hot, gate, 0.0), axis=1, keepdims=True)
            hotf = hot.astype(F32)
            hotb = hotf.astype(BF16)
            picks.append((hotb, gsel, jnp.transpose(hotf).astype(BF16)))
            at = pl.ds(base + i * cap, cap)

            def gather(j, _, o=o, q=q, hotb=hotb, at=at):
                cols = pl.ds(pl.multiple_of(j * tile, tile), tile)
                R[at, cols] = jnp.dot(
                    hotb, TOK[o, q, :, cols], preferred_element_type=F32
                ).astype(BF16)
                return 0

            lax.fori_loop(0, width // tile, gather, 0)
        span = pl.ds(base, cap * len(blocks))
        pre = jnp.dot(R[span, :], WC[...], preferred_element_type=F32)
        return picks, pre

    def cot_part(blocks, base, picks, pre, leave):
        def gather(j, _):
            cols = pl.ds(pl.multiple_of(j * tile, tile), tile)
            for i, (o, q) in enumerate(blocks):
                S[pl.ds(base + i * cap, cap), cols] = (
                    picks[i][1]
                    * jnp.dot(picks[i][0], COT[o, q, :, cols], preferred_element_type=F32)
                ).astype(BF16)
            return 0

        lax.fori_loop(0, width // tile, gather, 0)
        span = pl.ds(base, cap * len(blocks))
        back = lax.dot_general(S[span, :], WD[...], over_last, preferred_element_type=F32)
        gate_pre = pre[:, :hid]
        up_pre = pre[:, hid:]
        sigma = jax.nn.sigmoid(gate_pre)
        active = gate_pre * sigma
        H[span, :] = (active * up_pre).astype(BF16)
        GGU[span, pl.ds(0, hid)] = (
            back * up_pre * sigma * (1.0 + gate_pre * (1.0 - sigma))
        ).astype(BF16)
        GGU[span, pl.ds(hid, hid)] = (back * active).astype(BF16)

        def spread(j, _):
            cols = pl.ds(pl.multiple_of(j * tile, tile), tile)
            grads = lax.dot_general(
                GGU[span, :], WC[cols, :], over_last, preferred_element_type=F32
            ).astype(BF16)
            for i, (o, q) in enumerate(blocks):
                PART[o, q, :, cols] = jnp.dot(
                    picks[i][2], grads[i * cap : (i + 1) * cap], preferred_element_type=F32
                ).astype(BF16)
            return 0

        for w in (0, 1):
            lax.fori_loop(2 * w, 2 * w + 2, spread, 0)
            leave(w)

    def part_put(o, w):
        cols = pl.ds(w * (width // 2), width // 2)
        put(
            PART.at[o, 1, :, cols], SIB.at[o, :, cols], ps_send.at[o, w], ps_recv.at[o, w], sib
        )

    def part_take(o, halves=(0, 1)):
        for w in halves:
            cols = pl.ds(w * (width // 2), width // 2)
            arrived(SIB.at[o, :, cols], ps_send.at[o, w], ps_recv.at[o, w], sib)

    def sib_takes(arrays, s):
        for a in arrays:
            if s == 0:
                arrived(bufs[a].at[0, 1], sib_send.at[a, 0], sib_recv.at[a, 0], sib)
            else:
                for d in (0, 1):
                    sib_take(a, d, s)

    def blocks_of(s):
        if s == 0:
            return (0,), 0
        return ((n - s, s) if s < half else (half,)), 2 * cap + (s - 1) * 4 * cap

    def tokens_of(s):
        sib_takes((2, 3, 0), s)
        offs, base = blocks_of(s)
        return token_part([(o, q) for o in offs for q in (0, 1)], base)

    def rest_of(s, picks, pre, between=None):
        sib_takes((1,), s)
        offs, base = blocks_of(s)

        def leave(w):
            for o in offs:
                part_put(o, w)
            if between is not None and w == 0:
                between()

        cot_part([(o, q) for o in offs for q in (0, 1)], base, picks, pre, leave)

    def batch(s):
        if s == 0:
            for cp in local + weights:
                cp.wait()
        rest_of(s, *tokens_of(s))

    for cp in local + weights:
        cp.wait()
    rest_of(0, *tokens_of(0))
    for s in range(1, half):
        for a in (2, 3, 0):
            for d in (0, 1):
                ring_take(a, d, s)
        ready = tokens_of(s)
        for d in (0, 1):
            ring_take(1, d, s)
        rest_of(s, *ready)
    for a in (2, 3, 0):
        for d in (0, 1):
            ring_take(a, d, half)

    def rs_dst(d, j, h):
        return RB.at[d, j - 1, pl.ds(h // 2 * hr, hr), pl.ds(h % 2 * hw, hw)]

    def rs_send_piece(d, j, h):
        k = half - j + 1
        o = k if d == 0 else n - k
        add = j > 2 or (j == 2 and h // 2 == d)
        if add:
            arrived(rs_dst(d, j - 1, h), rs_send.at[d, j - 2, h], rs_recv.at[d, j - 2, h], nxt[d])

        cols = pl.ds(h % 2 * hw, hw)

        def add_rows(i, _):
            r = pl.ds(pl.multiple_of(h // 2 * hr + i * 16, 16), 16)
            total = PART[o, 0, r, cols].astype(F32) + SIB[o, r, cols].astype(F32)
            if add:
                total = total + RB[d, j - 2, r, cols].astype(F32)
            PART[o, 0, r, cols] = total.astype(BF16)
            return 0

        lax.fori_loop(0, hr // 16, add_rows, 0)
        put(
            PART.at[o, 0, pl.ds(h // 2 * hr, hr), cols], rs_dst(d, j, h),
            rs_send.at[d, j - 1, h], rs_recv.at[d, j - 1, h], nxt[d],
        )

    def early_half(j, h):
        for d in (0, 1):
            rs_send_piece(d, j, 2 * (1 - d) + h)

    def early(j):
        for h in (0, 1):
            early_half(j, h)

    def late(j):
        for h in (0, 1):
            for d in (0, 1):
                rs_send_piece(d, j, 2 * d + h)

    def down_grad():
        def body(j, _):
            cols = pl.ds(pl.multiple_of(j * tile, tile), tile)
            out_down[0, :, cols] = lax.dot_general(
                H[...], S[:, cols], over_rows, preferred_element_type=F32
            ).astype(BF16)
            return 0

        lax.fori_loop(0, width // tile, body, 0)

    wt = width // 8

    def in_grads(lo, hi):
        def body(j, _):
            cols = pl.ds(pl.multiple_of(j * wt, wt), wt)
            both = lax.dot_general(R[:, cols], GGU[...], over_rows, preferred_element_type=F32)
            out_gate[0, cols, :] = both[:, :hid].astype(BF16)
            out_up[0, cols, :] = both[:, hid:].astype(BF16)
            return 0

        lax.fori_loop(lo, hi, body, 0)

    for o in range(n):
        if o not in (0, half):
            part_take(o)
    early(2)
    last = tokens_of(half)
    for d in (0, 1):
        ring_take(1, d, half)
    rest_of(half, *last, functools.partial(early_half, 3, 0))
    early_half(3, 1)
    for h in (0, 1):
        part_take(half, (h,))
        for d in (0, 1):
            rs_send_piece(d, 1, 2 * d + h)
    down_grad()
    in_grads(0, 1)
    for j in range(2, half + 1):
        late(j)
        if j + 2 <= half:
            early(j + 2)
        lo = 1 + 7 * (j - 2) // (half - 1)
        in_grads(lo, 1 + 7 * (j - 1) // (half - 1))
    part_take(0)

    def landed(d, h):
        arrived(
            rs_dst(d, half, h), rs_send.at[d, half - 1, h], rs_recv.at[d, half - 1, h], nxt[d]
        )

    for d in (0, 1):
        for h in (0, 1):
            landed(d, 2 * (1 - d) + h)
    for h in (0, 1):
        for d in (0, 1):
            landed(d, 2 * d + h)

            def final(i, _, d=d, h=h):
                cols = pl.ds(h * hw, hw)
                r = pl.ds(pl.multiple_of(d * hr + i * 16, 16), 16)
                total = PART[0, 0, r, cols].astype(F32) + SIB[0, r, cols].astype(F32)
                total = total + RB[0, half - 1, r, cols].astype(F32)
                total = total + RB[1, half - 1, r, cols].astype(F32)
                out_tok[r, cols] = total.astype(BF16)
                return 0

            lax.fori_loop(0, hr // 16, final, 0)
    for cp in sends:
        cp.wait_send()


def gathered(tokens, cotangent, routes, gates, helper, w_gate, w_up, w_down):
    rows, width = tokens.shape
    n = lax.axis_size("expert")
    devices = n * lax.axis_size("dp")
    hid = w_gate.shape[2]
    cap = 2 * rows * routes.shape[1] // devices
    home = cap - 3 * cap // 8
    half = n // 2
    slots = devices * cap
    top = routes.shape[1]
    anyw = pl.BlockSpec(memory_space=pl.ANY)
    vmem = pl.BlockSpec(memory_space=pltpu.VMEM)
    dma = pltpu.SemaphoreType.DMA
    return pl.pallas_call(
        functools.partial(ring_kernel, n, cap, home),
        out_shape=(
            pltpu.VMEM((rows, width), BF16),
            pltpu.VMEM((1, width, hid), BF16),
            pltpu.VMEM((1, width, hid), BF16),
            pltpu.VMEM((1, hid, width), BF16),
        ),
        in_specs=[anyw] * 8,
        out_specs=(vmem, vmem, vmem, vmem),
        scratch_shapes=[
            pltpu.VMEM((n, 2, rows, width), BF16),
            pltpu.VMEM((n, 2, rows, width), BF16),
            pltpu.VMEM((n, 2, top, rows), jnp.int32),
            pltpu.VMEM((n, 2, top, rows), F32),
            pltpu.VMEM((1, devices), jnp.int32),
            pltpu.VMEM((width, 2 * hid), BF16),
            pltpu.VMEM((hid, width), BF16),
            pltpu.VMEM((slots, width), BF16),
            pltpu.VMEM((slots, width), BF16),
            pltpu.VMEM((slots, hid), BF16),
            pltpu.VMEM((slots, 2 * hid), BF16),
            pltpu.VMEM((n, 2, rows, width), BF16),
            pltpu.VMEM((n, rows, width), BF16),
            pltpu.VMEM((2, half, rows, width), BF16),
            dma((5,)),
            dma((3,)),
            dma((4, 2, half)),
            dma((4, 2, half)),
            dma((4, 2 * half + 1)),
            dma((4, 2 * half + 1)),
            dma((n, 2)),
            dma((n, 2)),
            dma((2, half, 4)),
            dma((2, half, 4)),
        ],
        compiler_params=pltpu.CompilerParams(
            collective_id=0, has_side_effects=True, vmem_limit_bytes=56 * 1024 * 1024
        ),
    )(tokens, cotangent, routes.T, gates.T, helper[None], w_gate[0], w_up[0], w_down[0])


def flush_kernel(*refs):
    count = len(refs) // 2
    sems = refs[-1]
    copies = []
    for i in range(count):
        rows = refs[i].shape[-2]
        parts = 4 if rows % 64 == 0 else 1
        for k in range(parts):
            at = pl.ds(k * (rows // parts), rows // parts)
            at = (at,) if len(refs[i].shape) == 2 else (0, at)
            copies.append(
                pltpu.make_async_copy(refs[i].at[at], refs[count + i].at[at], sems.at[i, k])
            )
    for cp in copies:
        cp.start()
    for cp in copies:
        cp.wait()


def flush(*arrays):
    return pl.pallas_call(
        flush_kernel,
        out_shape=tuple(jax.ShapeDtypeStruct(a.shape, a.dtype) for a in arrays),
        in_specs=[pl.BlockSpec(memory_space=pltpu.VMEM)] * len(arrays),
        out_specs=tuple(pl.BlockSpec(memory_space=pl.ANY) for _ in arrays),
        scratch_shapes=[pltpu.SemaphoreType.DMA((len(arrays), 4))],
        compiler_params=pltpu.CompilerParams(vmem_limit_bytes=1024 * 1024),
    )(*arrays)


def plan(tokens, cotangent, routes, *rest):
    rows = tokens.shape[0]
    n, cores = lax.axis_size("expert"), lax.axis_size("dp")
    slots = 2 * rows * routes.shape[1]
    few = cores == 2 and n % 2 == 0 and n >= 6 and rows % 64 == 0 and n * cores * rows <= 2 * slots
    if few:
        return flush(*gathered(tokens, cotangent, routes, *rest))
    return local(tokens, cotangent, routes, *rest)


def solution(mesh):
    return jax.shard_map(
        plan,
        mesh=mesh,
        in_specs=(
            P(("groups", "expert", "dp"), None),
            P(("groups", "expert", "dp"), None),
            P(("groups", "expert", "dp"), None),
            P(("groups", "expert", "dp"), None),
            P("groups"),
            P(("expert", "dp"), None, None),
            P(("expert", "dp"), None, None),
            P(("expert", "dp"), None, None),
        ),
        out_specs=(
            P(("groups", "expert", "dp"), None),
            P(("groups", "expert", "dp"), None, None),
            P(("groups", "expert", "dp"), None, None),
            P(("groups", "expert", "dp"), None, None),
        ),
        check_vma=False,
    )
```
